256 devices in a mesh: tm: 256 (over y, z, x, core).
Axes of the slice: x: 4, y: 4, z: 8, core: 2. Of those that a mesh axis runs over, the one named last changes fastest.
Arguments:
- step_ops: float32 [512, 256, 256], P('tm')
- sources: float32 [512, 256], P('tm'), may hold values from -0.3 to 0.3
- terminal: float32 [256], replicated, may hold values from -6 to 6
- inertia_jac: float32 [512, 64], P('tm')
- gen_bus: int32 [64], replicated, may hold values from 0 to 255, as said below
Outputs:
- adjoint_states: float32 [512, 256], P('tm')
- sensitivity: float32 [64], replicated
The draws below stay inside these ranges and needn't reach their ends.
Inputs may be any that keep to these rules, and one draw needn't show every extreme that they name: `gen_bus`: the 64 entries are distinct state indices.
All inputs are finite; a program needn't handle non-finite values.
Results may differ from the reference program's by a relative error of at most 0.0003.
Values sent between devices are 32-bit elements; how exact they have to be, the bound alone decides.
No kernel may reach another device: no remote copies, remote signals or barrier semaphores. Data moves between devices by JAX's collectives and lax.ppermute only.
A program may use at most 256 MiB of HBM per device.

```python
import jax
import jax.numpy as jnp
from jax import lax

NS = 256
NGEN = 64
TIME_STEP_COUNT = 512


def draw_step_ops(key, part):
    row_couples = NS // 2
    baseline_level = jax.random.fold_in(key, 11)
    slow_share = 0.5
    sluggish_mask = jax.random.uniform(jax.random.fold_in(baseline_level, 1), (row_couples,)) < slow_share
    slow_rate = jnp.exp(jax.random.uniform(jax.random.fold_in(baseline_level, 2), (row_couples,), minval=jnp.log(0.05), maxval=jnp.log(0.4))) / TIME_STEP_COUNT
    fast_rate = jax.random.uniform(jax.random.fold_in(baseline_level, 3), (row_couples,), minval=1.0 / 50.0, maxval=1.0 / 30.0)
    rate = jnp.where(sluggish_mask, slow_rate, fast_rate)
    spike_step_list = jax.random.randint(jax.random.fold_in(baseline_level, 4), (2,), 0, TIME_STEP_COUNT)
    spike_retained = jax.random.uniform(jax.random.fold_in(baseline_level, 5), (2, row_couples), minval=0.55, maxval=0.8)
    rows = lax.broadcasted_iota(jnp.int32, (NS, NS), 0)
    cols = lax.broadcasted_iota(jnp.int32, (NS, NS), 1)
    pair_of_row = rows // 2
    odd_row = rows % 2
    partner = rows + 1 - 2 * odd_row
    sign = (2 * odd_row - 1).astype(jnp.float32)

    def one_step(time_increment):
        step_key = jax.random.fold_in(key, time_increment + 1000)
        factor = jnp.exp(jax.random.uniform(jax.random.fold_in(step_key, 1), (row_couples,), minval=0.0, maxval=jnp.log(2.0)))
        damping_factor = jnp.exp(-rate * factor)
        spike_event = jnp.ones((row_couples,), jnp.float32)
        spike_event = jnp.where((spike_step_list[0] == time_increment) & sluggish_mask, spike_retained[0], spike_event)
        spike_event = jnp.where((spike_step_list[1] == time_increment) & sluggish_mask, spike_event * spike_retained[1], spike_event)
        damping_factor = damping_factor * spike_event
        angle = jax.random.uniform(jax.random.fold_in(step_key, 2), (row_couples,), minval=-1.0, maxval=1.0)
        dec_rows = damping_factor[pair_of_row]
        ang_rows = angle[pair_of_row]
        on_diag = jnp.where(rows == cols, dec_rows * jnp.cos(ang_rows), 0.0)
        on_pair = jnp.where(cols == partner, sign * dec_rows * jnp.sin(ang_rows), 0.0)
        noise = jax.random.normal(jax.random.fold_in(step_key, 3), (NS, NS), jnp.float32) * (0.025 / NS ** 0.5)
        return (on_diag + on_pair + noise).astype(jnp.float32)
    return lax.map(one_step, jnp.arange(TIME_STEP_COUNT, dtype=jnp.int32))


def draw_inertia_jac(key, part):
    times = lax.broadcasted_iota(jnp.float32, (TIME_STEP_COUNT, NGEN), 0)
    ramp = 1.0 + 2.0 * times / (TIME_STEP_COUNT - 1)
    values = jnp.clip(jax.random.normal(jax.random.fold_in(key, 7), (TIME_STEP_COUNT, NGEN), jnp.float32), -4.0, 4.0)
    return (values * ramp).astype(jnp.float32)


def draw_gen_bus(key, part):
    inner = jax.random.permutation(jax.random.fold_in(key, 9), NS - 2).astype(jnp.int32) + 1
    ends = jnp.array([0, NS - 1], dtype=jnp.int32)
    chosen = jnp.concatenate([ends, inner[:NGEN - 2]], axis=0)
    order = jax.random.permutation(jax.random.fold_in(key, 10), NGEN)
    return chosen[order].astype(jnp.int32)


def block_scale(key, dims, cuts, low, high):
    level, own = 1.0, jax.random.fold_in(key, 6)
    for axis_at, blocks in cuts:
        steps = jnp.exp(jax.random.uniform(jax.random.fold_in(own, axis_at), (blocks,), jnp.float32, low / len(cuts), high / len(cuts)))
        level = level * jnp.repeat(steps, dims[axis_at] // blocks).reshape([-1 if axis == axis_at else 1 for axis in range(len(dims))])
    return level


def gaussian(key, extent, deviation, bound, pieces=(), held_as=jnp.bfloat16):
    drawn = deviation * jax.random.normal(key, extent, jnp.float32)
    if pieces:
        drawn = drawn * block_scale(key, extent, pieces, -0.22, 0.18)
    return jnp.clip(drawn, -bound, bound).astype(held_as)


def setup_inputs(seed: int = 0) -> dict:
    key_of = jax.random.split(jax.random.key(seed), 6)
    return {
        "step_ops": draw_step_ops(jax.random.fold_in(key_of[5], 71), 0),
        "sources": gaussian(key_of[1], (TIME_STEP_COUNT, NS), 0.05, 0.3, ((0, 256),), jnp.float32),
        "terminal": gaussian(key_of[2], (NS,), 1.0, 6.0, (), jnp.float32),
        "inertia_jac": draw_inertia_jac(jax.random.fold_in(key_of[5], 71), 0),
        "gen_bus": draw_gen_bus(jax.random.fold_in(key_of[5], 71), 0),
    }


def reference(step_ops, sources, terminal, inertia_jac, gen_bus):
    def back_step(lam, pair):
        oper, src = pair
        new = jnp.dot(oper, lam, precision=lax.Precision.HIGHEST, preferred_element_type=jnp.float32) + src
        return new, new

    last, adjoint_states = lax.scan(back_step, terminal, (step_ops, sources), reverse=True)
    picked = adjoint_states[:, gen_bus]
    total_steps = adjoint_states.shape[0]
    sensitivity = jnp.sum(picked * inertia_jac, axis=0) * (float(total_steps) ** -0.5)
    return adjoint_states, sensitivity
```

```python
import functools

import jax
import jax.numpy as jnp
from jax import lax
from jax.experimental import pallas as pl
from jax.experimental.pallas import tpu as pltpu
from jax.sharding import PartitionSpec as P


NY, NZ, NX, NC = 4, 8, 4, 2
N = 256
G = 64
MS = N + G
V = MS
C = MS + 8
ROWS = MS + 16
HALF = ROWS // 2
W_ROWS = 2 * N + 16
F32 = jnp.float32
VM = pl.BlockSpec(memory_space=pltpu.VMEM)


def place(index):
    core = lax.rem(index, NC)
    x = lax.rem(lax.div(index, NC), NX)
    z = lax.rem(lax.div(index, NC * NX), NZ)
    y = lax.div(index, NC * NX * NZ)
    return y, z, x, core


def pairs(move):
    out = []
    for index in range(NY * NZ * NX * NC):
        y, z, x, c = index // 64, (index // 8) % 8, (index // 2) % 4, index % 2
        y, z, x, c = move(y, z, x, c)
        out.append((index, (((y % NY) * NZ + z % NZ) * NX + x % NX) * NC + c))
    return out


OTHER_CORE = pairs(lambda y, z, x, c: (y, z, x, 1 - c))
X_FROM = [pairs(lambda y, z, x, c, d=d: (y, z, x - d, c)) for d in (1, 2, 3)]
Y_FROM = [pairs(lambda y, z, x, c, d=d: (y - d, z, x, c)) for d in (1, 2, 3)]
Z_ONE = [pairs(lambda y, z, x, c: (y, z ^ 1, x, c))]
Z_FROM = [
    pairs(lambda y, z, x, c: (y, z - 2, x, c)),
    pairs(lambda y, z, x, c: (y, z ^ 5, x, c)),
    pairs(lambda y, z, x, c: (y, z + 2, x, c)),
]


def split(value):
    high = value.astype(jnp.bfloat16)
    low = (value - high.astype(F32)).astype(jnp.bfloat16)
    return high, low


def product(left, right):
    lh, ll = split(left)
    rh, rl = split(right)
    a = jnp.concatenate([lh, lh, ll], axis=1)
    b = jnp.concatenate([rh, rl, rh], axis=0)
    return jnp.dot(a, b, preferred_element_type=F32)


def times_row(matrix, row):
    p = matrix * row
    p = p[:, :128] + p[:, 128:]
    return jnp.sum(p.T, axis=0, keepdims=True)


def compose(early, late):
    (me, se, ve, ce), (ml, sl, vl, cl) = early, late
    p = product(jnp.concatenate([me, se], axis=0), ml)
    return (
        p[:N],
        p[N:] + sl,
        times_row(me, vl) + ve,
        times_row(se, vl) + ce + cl,
    )


def load(ref):
    return ref[0:N, :], ref[N:MS, :], ref[V : V + 1, :], ref[C : C + 1, 0:G]


def store(ref, value):
    m, s, v, c = value
    ref[0:N, :] = m
    ref[N:MS, :] = s
    ref[V : V + 8, :] = jnp.broadcast_to(v, (8, N))
    ref[C : C + 8, :] = jnp.zeros((8, N), F32)
    ref[C : C + 1, 0:G] = c


def store_half(half_ref, ref, core):
    half_ref[...] = ref[pl.ds(pl.multiple_of(core * HALF, 8), HALF), :]


def me():
    return place(lax.axis_index("tm"))


def leaf_kernel(a_ref, row_ref, t_ref):
    a0, a1 = a_ref[0], a_ref[1]
    s0, s1 = row_ref[0:1, :], row_ref[1:2, :]
    m = product(a0, a1)
    v = times_row(a0, s1) + s0
    eye = (
        lax.broadcasted_iota(jnp.int32, (G, G), 0)
        == lax.broadcasted_iota(jnp.int32, (G, G), 1)
    ).astype(F32)
    column = lambda row: jnp.sum(eye * row, axis=1, keepdims=True)
    as_row = lambda col: jnp.sum(eye * col, axis=0, keepdims=True)
    states = lax.broadcasted_iota(jnp.int32, (G, N), 1).astype(F32)
    chosen = jnp.where(states == column(row_ref[4:5, 0:G]), 1.0, 0.0)
    d0 = chosen * column(row_ref[2:3, 0:G])
    d1 = chosen * column(row_ref[3:4, 0:G])
    s = product(d0, m) + product(d1, a1)
    c = as_row(jnp.sum(d0 * v + d1 * s1, axis=1, keepdims=True))
    store(t_ref, (m, s, v, c))


def pick(first, a, b):
    return (
        tuple(jnp.where(first, p, q) for p, q in zip(a, b)),
        tuple(jnp.where(first, q, p) for p, q in zip(a, b)),
    )


def core_kernel(mine_ref, other_ref, t_ref, half_ref):
    core = me()[3]
    early, late = pick(core == 0, load(mine_ref), load(other_ref))
    store(t_ref, compose(early, late))
    store_half(half_ref, t_ref, core)


def pair_kernel(mine_ref, direct_ref, swapped_ref, t_ref, half_ref, other_ref):
    _, z, _, core = me()
    other_ref[pl.ds(pl.multiple_of(core * HALF, 8), HALF), :] = direct_ref[...]
    other_ref[pl.ds(pl.multiple_of((1 - core) * HALF, 8), HALF), :] = swapped_ref[...]
    first = lax.rem(z, 2) == 0
    early, late = pick(first, load(mine_ref), load(other_ref))
    store(t_ref, compose(early, late))
    store_half(half_ref, t_ref, core)


def fill(slots_ref, at, core, mine_ref, direct, swapped):
    slots_ref[at] = mine_ref[...]
    for d in (1, 2, 3):
        slot = lax.rem(at + d, 4)
        slots_ref[slot, pl.ds(pl.multiple_of(core * HALF, 8), HALF), :] = direct[d - 1][...]
        slots_ref[slot, pl.ds(pl.multiple_of((1 - core) * HALF, 8), HALF), :] = swapped[d - 1][...]


def quad_at(axis, z, x):
    return x if axis == "x" else lax.div(z, 2)


def quad_kernel(axis, mine_ref, d1, d2, d3, s1, s2, s3, t_ref, half_ref, slots_ref, tb_ref):
    _, z, x, core = me()
    fill(slots_ref, quad_at(axis, z, x), core, mine_ref, (d1, d2, d3), (s1, s2, s3))
    tb = compose(load(slots_ref.at[2]), load(slots_ref.at[3]))
    ta = compose(load(slots_ref.at[0]), load(slots_ref.at[1]))
    store(tb_ref, tb)
    store(t_ref, compose(ta, tb))
    store_half(half_ref, t_ref, core)


def extend(w_ref, late_m, late_v, out_ref):
    out_ref[0 : 2 * N, :] = product(w_ref[0 : 2 * N, :], late_m)
    for state in (0, 1):
        at = 2 * N + 8 * state
        offset = times_row(w_ref[N * state : N * (state + 1), :], late_v)
        out_ref[at : at + 8, :] = w_ref[at : at + 8, :] + offset


def own_core_kernel(t_ref, a_ref, row_ref, other_ref, out_ref, w_ref):
    w_ref[0:N, :] = t_ref[0:N, :]
    w_ref[N : 2 * N, :] = a_ref[1]
    w_ref[2 * N : 2 * N + 8, :] = t_ref[V : V + 8, :]
    w_ref[2 * N + 8 :, :] = jnp.broadcast_to(row_ref[1:2, :], (8, N))
    own_pair(me()[3], w_ref, other_ref, out_ref)


def own_pair_kernel(w_ref, late_ref, out_ref):
    own_pair(lax.rem(me()[1], 2), w_ref, late_ref, out_ref)


def own_pair(bit, w_ref, late_ref, out_ref):
    @pl.when(bit == 0)
    def _():
        extend(w_ref, late_ref[0:N, :], late_ref[V : V + 1, :], out_ref)

    @pl.when(bit != 0)
    def _():
        out_ref[...] = w_ref[...]


def own_quad_kernel(axis, w_ref, slots_ref, tb_ref, out_ref):
    _, z, x, _ = me()
    at = quad_at(axis, z, x)

    @pl.when(at == 0)
    def _():
        m1, v1 = slots_ref[1, 0:N, :], slots_ref[1, V : V + 1, :]
        late_m = product(m1, tb_ref[0:N, :])
        late_v = times_row(m1, tb_ref[V : V + 1, :]) + v1
        extend(w_ref, late_m, late_v, out_ref)

    @pl.when(at == 1)
    def _():
        extend(w_ref, tb_ref[0:N, :], tb_ref[V : V + 1, :], out_ref)

    @pl.when(at == 2)
    def _():
        extend(w_ref, slots_ref[3, 0:N, :], slots_ref[3, V : V + 1, :], out_ref)

    @pl.when(at == 3)
    def _():
        out_ref[...] = w_ref[...]


def last_kernel(scale, mine_ref, d1, d2, d3, s1, s2, s3, w_ref, end_ref, states_ref, sens_ref, slots_ref):
    y, _, _, core = me()
    fill(slots_ref, y, core, mine_ref, (d1, d2, d3), (s1, s2, s3))
    lam = end_ref[...]
    here = lam
    total = jnp.zeros((1, G), F32)
    for q in (3, 2, 1, 0):
        here = jnp.where(y == q, lam, here)
        m, s, v, c = load(slots_ref.at[q])
        total = total + times_row(s, lam) + c
        lam = times_row(m, lam) + v
    sens_ref[...] = total * scale
    for state in (0, 1):
        at = 2 * N + 8 * state
        states_ref[state : state + 1, :] = (
            times_row(w_ref[N * state : N * (state + 1), :], here) + w_ref[at : at + 1, :]
        )


def call(kernel, outs, args, scratch=(), products=1):
    shapes = [jax.ShapeDtypeStruct(o, F32) for o in outs]
    return pl.pallas_call(
        kernel,
        out_shape=shapes,
        in_specs=[VM] * len(args),
        out_specs=[VM] * len(outs),
        scratch_shapes=list(scratch),
        compiler_params=pltpu.CompilerParams(vmem_limit_bytes=16 << 20),
        cost_estimate=pl.CostEstimate(
            flops=products * 6 * MS * N * N, bytes_accessed=1 << 20, transcendentals=0
        ),
    )(*args)


def exchange(half, moves):
    direct, swapped = [], []
    for move in moves:
        direct.append(lax.ppermute(half, "tm", move))
    for part in direct:
        swapped.append(lax.ppermute(part, "tm", OTHER_CORE))
    return direct, swapped


def local(step_ops, sources, terminal, inertia_jac, gen_bus):
    t, h, w = (ROWS, N), (HALF, N), (W_ROWS, N)
    part = functools.partial
    wide = lambda rows: jnp.pad(rows, ((0, 0), (0, N - G)))
    rows = jnp.concatenate(
        [sources, wide(inertia_jac), wide(gen_bus.astype(F32).reshape(1, G)), jnp.zeros((3, N), F32)]
    )
    (leaf,) = call(leaf_kernel, [t], [step_ops, rows])
    total = leaf
    other = lax.ppermute(total, "tm", OTHER_CORE)
    total, half = call(core_kernel, [t, h], [total, other])

    direct, swapped = exchange(half, X_FROM)
    (own,) = call(own_core_kernel, [w], [leaf, step_ops, rows, other], scratch=[pltpu.VMEM(w, F32)])
    total, half, slots, tb = call(
        part(quad_kernel, "x"), [t, h, (4,) + t, t], [total, *direct, *swapped], products=3
    )

    direct, swapped = exchange(half, Z_ONE)
    (own,) = call(part(own_quad_kernel, "x"), [w], [own, slots, tb], products=2)
    total, half, late = call(pair_kernel, [t, h, t], [total, *direct, *swapped])

    direct, swapped = exchange(half, Z_FROM)
    (own,) = call(own_pair_kernel, [w], [own, late])
    total, half, slots, tb = call(
        part(quad_kernel, "z"), [t, h, (4,) + t, t], [total, *direct, *swapped], products=3
    )

    direct, swapped = exchange(half, Y_FROM)
    (own,) = call(part(own_quad_kernel, "z"), [w], [own, slots, tb], products=2)
    steps = step_ops.shape[0] * lax.axis_size("tm")
    states, sens = call(
        part(last_kernel, float(steps) ** -0.5),
        [(2, N), (1, G)],
        [total, *direct, *swapped, own, terminal.reshape(1, N)],
        scratch=[pltpu.VMEM((4,) + t, F32)],
    )
    return states, sens.reshape(G)


def solution(mesh):
    in_specs = (P("tm", None, None), P("tm", None), P(), P("tm", None), P())
    out_specs = (P("tm", None), P())
    return jax.shard_map(local, mesh=mesh, in_specs=in_specs, out_specs=out_specs, check_vma=False)
```

```python
import functools

import jax
import jax.numpy as jnp
from jax import lax
from jax.experimental import pallas as pl
from jax.experimental.pallas import tpu as pltpu
from jax.sharding import PartitionSpec as P


NY, NZ, NX, NC = 4, 8, 4, 2
N = 256
G = 64
MS = N + G
V = MS
C = MS + 8
ROWS = MS + 16
HALF = ROWS // 2
W_ROWS = 2 * N + 16
F32 = jnp.float32
VM = pl.BlockSpec(memory_space=pltpu.VMEM)


def place(index):
    core = lax.rem(index, NC)
    x = lax.rem(lax.div(index, NC), NX)
    z = lax.rem(lax.div(index, NC * NX), NZ)
    y = lax.div(index, NC * NX * NZ)
    return y, z, x, core


def pairs(move):
    out = []
    for index in range(NY * NZ * NX * NC):
        y, z, x, c = index // 64, (index // 8) % 8, (index // 2) % 4, index % 2
        y, z, x, c = move(y, z, x, c)
        out.append((index, (((y % NY) * NZ + z % NZ) * NX + x % NX) * NC + c))
    return out


OTHER_CORE = pairs(lambda y, z, x, c: (y, z, x, 1 - c))
X_FROM = (
    pairs(lambda y, z, x, c: (y, z, x + (1 if c else -1), c)),
    pairs(lambda y, z, x, c: (y, z, x + 2, c)),
)
Y_FROM = (
    pairs(lambda y, z, x, c: (y + (1 if c else -1), z, x, c)),
    pairs(lambda y, z, x, c: (y + 2, z, x, c)),
)
Z_ONE = pairs(lambda y, z, x, c: (y, z ^ 1, x, c))
Z_FROM = (
    pairs(lambda y, z, x, c: (y, z + (2 if c else -2), x, c)),
    pairs(lambda y, z, x, c: (y, z ^ 5, x, c)),
)


def split(value):
    high = value.astype(jnp.bfloat16)
    low = (value - high.astype(F32)).astype(jnp.bfloat16)
    return high, low


def product(left, right):
    lh, ll = split(left)
    rh, rl = split(right)
    a = jnp.concatenate([lh, lh, ll], axis=1)
    b = jnp.concatenate([rh, rl, rh], axis=0)
    return jnp.dot(a, b, preferred_element_type=F32)


def times_row(matrix, row):
    p = matrix * row
    p = p[:, :128] + p[:, 128:]
    return jnp.sum(p.T, axis=0, keepdims=True)


def compose(early, late):
    (me, se, ve, ce), (ml, sl, vl, cl) = early, late
    p = product(jnp.concatenate([me, se], axis=0), ml)
    return (
        p[:N],
        p[N:] + sl,
        times_row(me, vl) + ve,
        times_row(se, vl) + ce + cl,
    )


def load(ref):
    return ref[0:N, :], ref[N:MS, :], ref[V : V + 1, :], ref[C : C + 1, 0:G]


def store(ref, value):
    m, s, v, c = value
    ref[0:N, :] = m
    ref[N:MS, :] = s
    ref[V : V + 8, :] = jnp.broadcast_to(v, (8, N))
    ref[C : C + 8, :] = jnp.zeros((8, N), F32)
    ref[C : C + 1, 0:G] = c


def store_half(half_ref, ref, core):
    half_ref[...] = ref[pl.ds(pl.multiple_of(core * HALF, 8), HALF), :]


def me():
    return place(lax.axis_index("tm"))


def leaf_kernel(a_ref, row_ref, t_ref):
    a0, a1 = a_ref[0], a_ref[1]
    s0, s1 = row_ref[0:1, :], row_ref[1:2, :]
    m = product(a0, a1)
    v = times_row(a0, s1) + s0
    eye = (
        lax.broadcasted_iota(jnp.int32, (G, G), 0)
        == lax.broadcasted_iota(jnp.int32, (G, G), 1)
    ).astype(F32)
    column = lambda row: jnp.sum(eye * row, axis=1, keepdims=True)
    as_row = lambda col: jnp.sum(eye * col, axis=0, keepdims=True)
    states = lax.broadcasted_iota(jnp.int32, (G, N), 1).astype(F32)
    chosen = jnp.where(states == column(row_ref[4:5, 0:G]), 1.0, 0.0)
    d0 = chosen * column(row_ref[2:3, 0:G])
    d1 = chosen * column(row_ref[3:4, 0:G])
    s = product(d0, m) + product(d1, a1)
    c = as_row(jnp.sum(d0 * v + d1 * s1, axis=1, keepdims=True))
    store(t_ref, (m, s, v, c))


def pick(first, a, b):
    return (
        tuple(jnp.where(first, p, q) for p, q in zip(a, b)),
        tuple(jnp.where(first, q, p) for p, q in zip(a, b)),
    )


def core_kernel(mine_ref, other_ref, t_ref, half_ref):
    core = me()[3]
    early, late = pick(core == 0, load(mine_ref), load(other_ref))
    store(t_ref, compose(early, late))
    store_half(half_ref, t_ref, core)


def pair_kernel(mine_ref, direct_ref, swapped_ref, t_ref, half_ref, other_ref):
    _, z, _, core = me()
    other_ref[pl.ds(pl.multiple_of(core * HALF, 8), HALF), :] = direct_ref[...]
    other_ref[pl.ds(pl.multiple_of((1 - core) * HALF, 8), HALF), :] = swapped_ref[...]
    first = lax.rem(z, 2) == 0
    early, late = pick(first, load(mine_ref), load(other_ref))
    store(t_ref, compose(early, late))
    store_half(half_ref, t_ref, core)


def fill(slots_ref, at, core, mine_ref, side_ref, other_side_ref, far_ref, other_far_ref):
    slots_ref[at] = mine_ref[...]
    slots_ref[lax.rem(at + 1 + 2 * core, 4)] = side_ref[...]
    slots_ref[lax.rem(at + 3 - 2 * core, 4)] = other_side_ref[...]
    far = lax.rem(at + 2, 4)
    slots_ref[far, pl.ds(pl.multiple_of(core * HALF, 8), HALF), :] = far_ref[...]
    slots_ref[far, pl.ds(pl.multiple_of((1 - core) * HALF, 8), HALF), :] = other_far_ref[...]


def quad_at(axis, z, x):
    return x if axis == "x" else lax.div(z, 2)


def quad_kernel(axis, mine_ref, a, b, c, d, t_ref, half_ref, slots_ref, tb_ref):
    _, z, x, core = me()
    fill(slots_ref, quad_at(axis, z, x), core, mine_ref, a, b, c, d)
    tb = compose(load(slots_ref.at[2]), load(slots_ref.at[3]))
    ta = compose(load(slots_ref.at[0]), load(slots_ref.at[1]))
    store(tb_ref, tb)
    store(t_ref, compose(ta, tb))
    store_half(half_ref, t_ref, core)


def extend(w_ref, late_m, late_v, out_ref):
    out_ref[0 : 2 * N, :] = product(w_ref[0 : 2 * N, :], late_m)
    for state in (0, 1):
        at = 2 * N + 8 * state
        offset = times_row(w_ref[N * state : N * (state + 1), :], late_v)
        out_ref[at : at + 8, :] = w_ref[at : at + 8, :] + offset


def own_core_kernel(t_ref, a_ref, row_ref, other_ref, out_ref, w_ref):
    w_ref[0:N, :] = t_ref[0:N, :]
    w_ref[N : 2 * N, :] = a_ref[1]
    w_ref[2 * N : 2 * N + 8, :] = t_ref[V : V + 8, :]
    w_ref[2 * N + 8 :, :] = jnp.broadcast_to(row_ref[1:2, :], (8, N))
    own_pair(me()[3], w_ref, other_ref, out_ref)


def own_pair_kernel(w_ref, late_ref, out_ref):
    own_pair(lax.rem(me()[1], 2), w_ref, late_ref, out_ref)


def own_pair(bit, w_ref, late_ref, out_ref):
    @pl.when(bit == 0)
    def _():
        extend(w_ref, late_ref[0:N, :], late_ref[V : V + 1, :], out_ref)

    @pl.when(bit != 0)
    def _():
        out_ref[...] = w_ref[...]


def own_quad_kernel(axis, w_ref, slots_ref, tb_ref, out_ref):
    _, z, x, _ = me()
    at = quad_at(axis, z, x)

    @pl.when(at == 0)
    def _():
        m1, v1 = slots_ref[1, 0:N, :], slots_ref[1, V : V + 1, :]
        late_m = product(m1, tb_ref[0:N, :])
        late_v = times_row(m1, tb_ref[V : V + 1, :]) + v1
        extend(w_ref, late_m, late_v, out_ref)

    @pl.when(at == 1)
    def _():
        extend(w_ref, tb_ref[0:N, :], tb_ref[V : V + 1, :], out_ref)

    @pl.when(at == 2)
    def _():
        extend(w_ref, slots_ref[3, 0:N, :], slots_ref[3, V : V + 1, :], out_ref)

    @pl.when(at == 3)
    def _():
        out_ref[...] = w_ref[...]


def last_kernel(scale, mine_ref, a, b, c, d, w_ref, end_ref, states_ref, sens_ref, slots_ref):
    y, _, _, core = me()
    fill(slots_ref, y, core, mine_ref, a, b, c, d)
    lam = end_ref[...]
    here = lam
    total = jnp.zeros((1, G), F32)
    for q in (3, 2, 1, 0):
        here = jnp.where(y == q, lam, here)
        m, s, v, const = load(slots_ref.at[q])
        total = total + times_row(s, lam) + const
        lam = times_row(m, lam) + v
    sens_ref[...] = total * scale
    for state in (0, 1):
        at = 2 * N + 8 * state
        states_ref[state : state + 1, :] = (
            times_row(w_ref[N * state : N * (state + 1), :], here) + w_ref[at : at + 1, :]
        )


def call(kernel, outs, args, scratch=(), products=1):
    shapes = [jax.ShapeDtypeStruct(o, F32) for o in outs]
    return pl.pallas_call(
        kernel,
        out_shape=shapes,
        in_specs=[VM] * len(args),
        out_specs=[VM] * len(outs),
        scratch_shapes=list(scratch),
        compiler_params=pltpu.CompilerParams(vmem_limit_bytes=16 << 20),
        cost_estimate=pl.CostEstimate(
            flops=products * 6 * MS * N * N, bytes_accessed=1 << 20, transcendentals=0
        ),
    )(*args)


def send(value, move):
    return lax.ppermute(value, "tm", move)


def gather(whole, half, moves):
    side, far = send(whole, moves[0]), send(half, moves[1])
    return side, send(side, OTHER_CORE), far, send(far, OTHER_CORE)


def local(step_ops, sources, terminal, inertia_jac, gen_bus):
    t, h, w = (ROWS, N), (HALF, N), (W_ROWS, N)
    part = functools.partial
    wide = lambda rows: jnp.pad(rows, ((0, 0), (0, N - G)))
    rows = jnp.concatenate(
        [sources, wide(inertia_jac), wide(gen_bus.astype(F32).reshape(1, G)), jnp.zeros((3, N), F32)]
    )
    (leaf,) = call(leaf_kernel, [t], [step_ops, rows])
    total = leaf
    other = send(total, OTHER_CORE)
    total, half = call(core_kernel, [t, h], [total, other])

    parts = gather(total, half, X_FROM)
    (own,) = call(own_core_kernel, [w], [leaf, step_ops, rows, other], scratch=[pltpu.VMEM(w, F32)])
    total, half, slots, tb = call(
        part(quad_kernel, "x"), [t, h, (4,) + t, t], [total, *parts], products=3
    )

    direct = send(half, Z_ONE)
    swapped = send(direct, OTHER_CORE)
    (own,) = call(part(own_quad_kernel, "x"), [w], [own, slots, tb], products=2)
    total, half, late = call(pair_kernel, [t, h, t], [total, direct, swapped])

    parts = gather(total, half, Z_FROM)
    (own,) = call(own_pair_kernel, [w], [own, late])
    total, half, slots, tb = call(
        part(quad_kernel, "z"), [t, h, (4,) + t, t], [total, *parts], products=3
    )

    parts = gather(total, half, Y_FROM)
    (own,) = call(part(own_quad_kernel, "z"), [w], [own, slots, tb], products=2)
    steps = step_ops.shape[0] * lax.axis_size("tm")
    states, sens = call(
        part(last_kernel, float(steps) ** -0.5),
        [(2, N), (1, G)],
        [total, *parts, own, terminal.reshape(1, N)],
        scratch=[pltpu.VMEM((4,) + t, F32)],
    )
    return states, sens.reshape(G)


def solution(mesh):
    in_specs = (P("tm", None, None), P("tm", None), P(), P("tm", None), P())
    out_specs = (P("tm", None), P())
    return jax.shard_map(local, mesh=mesh, in_specs=in_specs, out_specs=out_specs, check_vma=False)
```

```python
import functools

import jax
import jax.numpy as jnp
from jax import lax
from jax.experimental import pallas as pl
from jax.experimental.pallas import tpu as pltpu
from jax.sharding import PartitionSpec as P


NY, NZ, NX, NC = 4, 8, 4, 2
N = 256
G = 64
MS = N + G
V = MS
C = MS + 8
ROWS = MS + 16
HALF = ROWS // 2
QUARTER = 88
MEET = HALF - QUARTER
W_ROWS = 2 * N + 16
F32 = jnp.float32
VM = pl.BlockSpec(memory_space=pltpu.VMEM)


def place(index):
    core = lax.rem(index, NC)
    x = lax.rem(lax.div(index, NC), NX)
    z = lax.rem(lax.div(index, NC * NX), NZ)
    y = lax.div(index, NC * NX * NZ)
    return y, z, x, core


def pairs(move):
    out = []
    for index in range(NY * NZ * NX * NC):
        y, z, x, c = index // 64, (index // 8) % 8, (index // 2) % 4, index % 2
        y, z, x, c = move(y, z, x, c)
        out.append((index, (((y % NY) * NZ + z % NZ) * NX + x % NX) * NC + c))
    return out


OTHER_CORE = pairs(lambda y, z, x, c: (y, z, x, 1 - c))
X_FROM = (
    pairs(lambda y, z, x, c: (y, z, x + (1 if c else -1), c)),
    pairs(lambda y, z, x, c: (y, z, x + 2, c)),
)
Y_FROM = (
    pairs(lambda y, z, x, c: (y + (1 if c else -1), z, x, c)),
    pairs(lambda y, z, x, c: (y + 2, z, x, c)),
)
Z_ONE = pairs(lambda y, z, x, c: (y, z ^ 1, x, c))
Z_SIDE = pairs(lambda y, z, x, c: (y, z + (1 if z % 2 else -1), x, c))
Z_FAR = pairs(lambda y, z, x, c: (y, z ^ 5, x, c))


def split(value):
    high = value.astype(jnp.bfloat16)
    low = (value - high.astype(F32)).astype(jnp.bfloat16)
    return high, low


def product(left, right):
    lh, ll = split(left)
    rh, rl = split(right)
    a = jnp.concatenate([lh, lh, ll], axis=1)
    b = jnp.concatenate([rh, rl, rh], axis=0)
    return jnp.dot(a, b, preferred_element_type=F32)


def times_row(matrix, row):
    p = matrix * row
    p = p[:, :128] + p[:, 128:]
    return jnp.sum(p.T, axis=0, keepdims=True)


def compose(early, late):
    (me, se, ve, ce), (ml, sl, vl, cl) = early, late
    p = product(jnp.concatenate([me, se], axis=0), ml)
    return (
        p[:N],
        p[N:] + sl,
        times_row(me, vl) + ve,
        times_row(se, vl) + ce + cl,
    )


def load(ref):
    return ref[0:N, :], ref[N:MS, :], ref[V : V + 1, :], ref[C : C + 1, 0:G]


def store(ref, value):
    m, s, v, c = value
    ref[0:N, :] = m
    ref[N:MS, :] = s
    ref[V : V + 8, :] = jnp.broadcast_to(v, (8, N))
    ref[C : C + 8, :] = jnp.zeros((8, N), F32)
    ref[C : C + 1, 0:G] = c


def store_half(half_ref, ref, core):
    half_ref[...] = ref[pl.ds(pl.multiple_of(core * HALF, 8), HALF), :]


def me():
    return place(lax.axis_index("tm"))


def leaf_kernel(a_ref, row_ref, t_ref):
    a0, a1 = a_ref[0], a_ref[1]
    s0, s1 = row_ref[0:1, :], row_ref[1:2, :]
    m = product(a0, a1)
    v = times_row(a0, s1) + s0
    eye = (
        lax.broadcasted_iota(jnp.int32, (G, G), 0)
        == lax.broadcasted_iota(jnp.int32, (G, G), 1)
    ).astype(F32)
    column = lambda row: jnp.sum(eye * row, axis=1, keepdims=True)
    as_row = lambda col: jnp.sum(eye * col, axis=0, keepdims=True)
    states = lax.broadcasted_iota(jnp.int32, (G, N), 1).astype(F32)
    chosen = jnp.where(states == column(row_ref[4:5, 0:G]), 1.0, 0.0)
    d0 = chosen * column(row_ref[2:3, 0:G])
    d1 = chosen * column(row_ref[3:4, 0:G])
    s = product(d0, m) + product(d1, a1)
    c = as_row(jnp.sum(d0 * v + d1 * s1, axis=1, keepdims=True))
    store(t_ref, (m, s, v, c))


def pick(first, a, b):
    return (
        tuple(jnp.where(first, p, q) for p, q in zip(a, b)),
        tuple(jnp.where(first, q, p) for p, q in zip(a, b)),
    )


def core_kernel(mine_ref, other_ref, t_ref, half_ref):
    core = me()[3]
    early, late = pick(core == 0, load(mine_ref), load(other_ref))
    store(t_ref, compose(early, late))
    store_half(half_ref, t_ref, core)


def pair_kernel(mine_ref, direct_ref, swapped_ref, t_ref, half_ref, quarter_ref, other_ref):
    _, z, _, core = me()
    other_ref[pl.ds(pl.multiple_of(core * HALF, 8), HALF), :] = direct_ref[...]
    other_ref[pl.ds(pl.multiple_of((1 - core) * HALF, 8), HALF), :] = swapped_ref[...]
    first = lax.rem(z, 2) == 0
    early, late = pick(first, load(mine_ref), load(other_ref))
    store(t_ref, compose(early, late))
    store_half(half_ref, t_ref, core)
    at = core * HALF + (1 - lax.rem(z, 2)) * MEET
    quarter_ref[...] = t_ref[pl.ds(pl.multiple_of(at, 8), QUARTER), :]


def fill_z(slots_ref, z, core, mine_ref, own_ref, got_ref, own_other_ref, got_other_ref):
    at, odd = lax.div(z, 2), lax.rem(z, 2)
    slots_ref[at] = mine_ref[...]
    far = lax.rem(at + 2, 4)
    for ref, parity, half in (
        (own_ref, odd, core),
        (got_ref, 1 - odd, core),
        (own_other_ref, odd, 1 - core),
        (got_other_ref, 1 - odd, 1 - core),
    ):
        side = lax.rem(at + 3 - 2 * parity, 4)
        row = half * HALF
        slots_ref[side, pl.ds(pl.multiple_of(row, 8), HALF), :] = ref[0:HALF, :]
        row = row + parity * MEET
        slots_ref[far, pl.ds(pl.multiple_of(row, 8), QUARTER), :] = ref[HALF : HALF + QUARTER, :]


def fill(slots_ref, at, core, mine_ref, side_ref, other_side_ref, far_ref, other_far_ref):
    slots_ref[at] = mine_ref[...]
    slots_ref[lax.rem(at + 1 + 2 * core, 4)] = side_ref[...]
    slots_ref[lax.rem(at + 3 - 2 * core, 4)] = other_side_ref[...]
    far = lax.rem(at + 2, 4)
    slots_ref[far, pl.ds(pl.multiple_of(core * HALF, 8), HALF), :] = far_ref[...]
    slots_ref[far, pl.ds(pl.multiple_of((1 - core) * HALF, 8), HALF), :] = other_far_ref[...]


def quad_at(axis, z, x):
    return x if axis == "x" else lax.div(z, 2)


def quad_kernel(axis, mine_ref, a, b, c, d, t_ref, half_ref, slots_ref, tb_ref):
    _, z, x, core = me()
    if axis == "x":
        fill(slots_ref, x, core, mine_ref, a, b, c, d)
    else:
        fill_z(slots_ref, z, core, mine_ref, a, b, c, d)
    tb = compose(load(slots_ref.at[2]), load(slots_ref.at[3]))
    ta = compose(load(slots_ref.at[0]), load(slots_ref.at[1]))
    store(tb_ref, tb)
    store(t_ref, compose(ta, tb))
    store_half(half_ref, t_ref, core)


def extend(w_ref, late_m, late_v, out_ref):
    out_ref[0 : 2 * N, :] = product(w_ref[0 : 2 * N, :], late_m)
    for state in (0, 1):
        at = 2 * N + 8 * state
        offset = times_row(w_ref[N * state : N * (state + 1), :], late_v)
        out_ref[at : at + 8, :] = w_ref[at : at + 8, :] + offset


def own_core_kernel(t_ref, a_ref, row_ref, other_ref, out_ref, w_ref):
    w_ref[0:N, :] = t_ref[0:N, :]
    w_ref[N : 2 * N, :] = a_ref[1]
    w_ref[2 * N : 2 * N + 8, :] = t_ref[V : V + 8, :]
    w_ref[2 * N + 8 :, :] = jnp.broadcast_to(row_ref[1:2, :], (8, N))
    own_pair(me()[3], w_ref, other_ref, out_ref)


def own_pair_kernel(w_ref, late_ref, out_ref):
    own_pair(lax.rem(me()[1], 2), w_ref, late_ref, out_ref)


def own_pair(bit, w_ref, late_ref, out_ref):
    @pl.when(bit == 0)
    def _():
        extend(w_ref, late_ref[0:N, :], late_ref[V : V + 1, :], out_ref)

    @pl.when(bit != 0)
    def _():
        out_ref[...] = w_ref[...]


def own_quad_kernel(axis, w_ref, slots_ref, tb_ref, out_ref):
    _, z, x, _ = me()
    at = quad_at(axis, z, x)

    @pl.when(at == 0)
    def _():
        m1, v1 = slots_ref[1, 0:N, :], slots_ref[1, V : V + 1, :]
        late_m = product(m1, tb_ref[0:N, :])
        late_v = times_row(m1, tb_ref[V : V + 1, :]) + v1
        extend(w_ref, late_m, late_v, out_ref)

    @pl.when(at == 1)
    def _():
        extend(w_ref, tb_ref[0:N, :], tb_ref[V : V + 1, :], out_ref)

    @pl.when(at == 2)
    def _():
        extend(w_ref, slots_ref[3, 0:N, :], slots_ref[3, V : V + 1, :], out_ref)

    @pl.when(at == 3)
    def _():
        out_ref[...] = w_ref[...]


def last_kernel(scale, mine_ref, a, b, c, d, w_ref, end_ref, states_ref, sens_ref, slots_ref):
    y, _, _, core = me()
    fill(slots_ref, y, core, mine_ref, a, b, c, d)
    lam = end_ref[...]
    here = lam
    total = jnp.zeros((1, G), F32)
    for q in (3, 2, 1, 0):
        here = jnp.where(y == q, lam, here)
        m, s, v, const = load(slots_ref.at[q])
        total = total + times_row(s, lam) + const
        lam = times_row(m, lam) + v
    sens_ref[...] = total * scale
    for state in (0, 1):
        at = 2 * N + 8 * state
        states_ref[state : state + 1, :] = (
            times_row(w_ref[N * state : N * (state + 1), :], here) + w_ref[at : at + 1, :]
        )


def call(kernel, outs, args, scratch=(), products=1):
    shapes = [jax.ShapeDtypeStruct(o, F32) for o in outs]
    return pl.pallas_call(
        kernel,
        out_shape=shapes,
        in_specs=[VM] * len(args),
        out_specs=[VM] * len(outs),
        scratch_shapes=list(scratch),
        compiler_params=pltpu.CompilerParams(vmem_limit_bytes=16 << 20),
        cost_estimate=pl.CostEstimate(
            flops=products * 6 * MS * N * N, bytes_accessed=1 << 20, transcendentals=0
        ),
    )(*args)


def send(value, move):
    return lax.ppermute(value, "tm", move)


def gather(whole, half, moves):
    side, far = send(whole, moves[0]), send(half, moves[1])
    return side, send(side, OTHER_CORE), far, send(far, OTHER_CORE)


def local(step_ops, sources, terminal, inertia_jac, gen_bus):
    t, h, w = (ROWS, N), (HALF, N), (W_ROWS, N)
    part = functools.partial
    wide = lambda rows: jnp.pad(rows, ((0, 0), (0, N - G)))
    rows = jnp.concatenate(
        [sources, wide(inertia_jac), wide(gen_bus.astype(F32).reshape(1, G)), jnp.zeros((3, N), F32)]
    )
    (leaf,) = call(leaf_kernel, [t], [step_ops, rows])
    total = leaf
    other = send(total, OTHER_CORE)
    total, half = call(core_kernel, [t, h], [total, other])

    parts = gather(total, half, X_FROM)
    (own,) = call(own_core_kernel, [w], [leaf, step_ops, rows, other], scratch=[pltpu.VMEM(w, F32)])
    total, half, slots, tb = call(
        part(quad_kernel, "x"), [t, h, (4,) + t, t], [total, *parts], products=3
    )

    direct = send(half, Z_ONE)
    swapped = send(direct, OTHER_CORE)
    (own,) = call(part(own_quad_kernel, "x"), [w], [own, slots, tb], products=2)
    total, half, quarter, late = call(
        pair_kernel, [t, h, (QUARTER, N), t], [total, direct, swapped]
    )

    far, side = send(quarter, Z_FAR), send(half, Z_SIDE)
    mine = jnp.concatenate([side, far])
    got = send(mine, Z_ONE)
    parts = mine, got, send(mine, OTHER_CORE), send(got, OTHER_CORE)
    (own,) = call(own_pair_kernel, [w], [own, late])
    total, half, slots, tb = call(
        part(quad_kernel, "z"), [t, h, (4,) + t, t], [total, *parts], products=3
    )

    parts = gather(total, half, Y_FROM)
    (own,) = call(part(own_quad_kernel, "z"), [w], [own, slots, tb], products=2)
    steps = step_ops.shape[0] * lax.axis_size("tm")
    states, sens = call(
        part(last_kernel, float(steps) ** -0.5),
        [(2, N), (1, G)],
        [total, *parts, own, terminal.reshape(1, N)],
        scratch=[pltpu.VMEM((4,) + t, F32)],
    )
    return states, sens.reshape(G)


def solution(mesh):
    in_specs = (P("tm", None, None), P("tm", None), P(), P("tm", None), P())
    out_specs = (P("tm", None), P())
    return jax.shard_map(local, mesh=mesh, in_specs=in_specs, out_specs=out_specs, check_vma=False)
```

```python
import functools

import jax
import jax.numpy as jnp
from jax import lax
from jax.experimental import pallas as pl
from jax.experimental.pallas import tpu as pltpu
from jax.sharding import PartitionSpec as P


NY, NZ, NX, NC = 4, 8, 4, 2
N = 256
G = 64
MS = N + G
V = MS
C = MS + 8
ROWS = MS + 16
HALF = ROWS // 2
W_ROWS = 2 * N + 16
F32 = jnp.float32
VM = pl.BlockSpec(memory_space=pltpu.VMEM)


def place(index):
    core = lax.rem(index, NC)
    x = lax.rem(lax.div(index, NC), NX)
    z = lax.rem(lax.div(index, NC * NX), NZ)
    y = lax.div(index, NC * NX * NZ)
    return y, z, x, core


def pairs(move):
    out = []
    for index in range(NY * NZ * NX * NC):
        y, z, x, c = index // 64, (index // 8) % 8, (index // 2) % 4, index % 2
        y, z, x, c = move(y, z, x, c)
        out.append((index, (((y % NY) * NZ + z % NZ) * NX + x % NX) * NC + c))
    return out


OTHER_CORE = pairs(lambda y, z, x, c: (y, z, x, 1 - c))
X_FROM = (
    pairs(lambda y, z, x, c: (y, z, x + (1 if c else -1), c)),
    pairs(lambda y, z, x, c: (y, z, x + 2, c)),
)
Y_FROM = (
    pairs(lambda y, z, x, c: (y + (1 if c else -1), z, x, c)),
    pairs(lambda y, z, x, c: (y + 2, z, x, c)),
)
Z_ONE = pairs(lambda y, z, x, c: (y, z ^ 1, x, c))
Z_SIDE = pairs(lambda y, z, x, c: (y, z + (1 if z % 2 else -1), x, c))
Z_FAR = pairs(lambda y, z, x, c: (y, z ^ 5, x, c))


def split(value):
    high = value.astype(jnp.bfloat16)
    low = (value - high.astype(F32)).astype(jnp.bfloat16)
    return high, low


def product(left, right):
    lh, ll = split(left)
    rh, rl = split(right)
    a = jnp.concatenate([lh, lh, ll], axis=1)
    b = jnp.concatenate([rh, rl, rh], axis=0)
    return jnp.dot(a, b, preferred_element_type=F32)


def times_row(matrix, row):
    p = matrix * row
    p = p[:, :128] + p[:, 128:]
    return jnp.sum(p.T, axis=0, keepdims=True)


def compose(early, late):
    (me, se, ve, ce), (ml, sl, vl, cl) = early, late
    p = product(jnp.concatenate([me, se], axis=0), ml)
    return (
        p[:N],
        p[N:] + sl,
        times_row(me, vl) + ve,
        times_row(se, vl) + ce + cl,
    )


def load(ref):
    return ref[0:N, :], ref[N:MS, :], ref[V : V + 1, :], ref[C : C + 1, 0:G]


def store(ref, value):
    m, s, v, c = value
    ref[0:N, :] = m
    ref[N:MS, :] = s
    ref[V : V + 8, :] = jnp.broadcast_to(v, (8, N))
    ref[C : C + 8, :] = jnp.zeros((8, N), F32)
    ref[C : C + 1, 0:G] = c


def store_half(half_ref, ref, core):
    half_ref[...] = ref[pl.ds(pl.multiple_of(core * HALF, 8), HALF), :]


def me():
    return place(lax.axis_index("tm"))


def leaf_kernel(a_ref, row_ref, t_ref):
    a0, a1 = a_ref[0], a_ref[1]
    s0, s1 = row_ref[0:1, :], row_ref[1:2, :]
    m = product(a0, a1)
    v = times_row(a0, s1) + s0
    eye = (
        lax.broadcasted_iota(jnp.int32, (G, G), 0)
        == lax.broadcasted_iota(jnp.int32, (G, G), 1)
    ).astype(F32)
    column = lambda row: jnp.sum(eye * row, axis=1, keepdims=True)
    as_row = lambda col: jnp.sum(eye * col, axis=0, keepdims=True)
    states = lax.broadcasted_iota(jnp.int32, (G, N), 1).astype(F32)
    chosen = jnp.where(states == column(row_ref[4:5, 0:G]), 1.0, 0.0)
    d0 = chosen * column(row_ref[2:3, 0:G])
    d1 = chosen * column(row_ref[3:4, 0:G])
    s = product(d0, m) + product(d1, a1)
    c = as_row(jnp.sum(d0 * v + d1 * s1, axis=1, keepdims=True))
    store(t_ref, (m, s, v, c))


def pick(first, a, b):
    return (
        tuple(jnp.where(first, p, q) for p, q in zip(a, b)),
        tuple(jnp.where(first, q, p) for p, q in zip(a, b)),
    )


def core_kernel(mine_ref, other_ref, t_ref, half_ref):
    core = me()[3]
    early, late = pick(core == 0, load(mine_ref), load(other_ref))
    store(t_ref, compose(early, late))
    store_half(half_ref, t_ref, core)


def pair_kernel(mine_ref, direct_ref, swapped_ref, t_ref, half_ref, other_ref):
    _, z, _, core = me()
    other_ref[pl.ds(pl.multiple_of(core * HALF, 8), HALF), :] = direct_ref[...]
    other_ref[pl.ds(pl.multiple_of((1 - core) * HALF, 8), HALF), :] = swapped_ref[...]
    first = lax.rem(z, 2) == 0
    early, late = pick(first, load(mine_ref), load(other_ref))
    store(t_ref, compose(early, late))
    store_half(half_ref, t_ref, core)


def fill_z(slots_ref, z, core, mine_ref, far_ref, other_far_ref, *sides):
    at, odd = lax.div(z, 2), lax.rem(z, 2)
    slots_ref[at] = mine_ref[...]
    first = pl.ds(pl.multiple_of(core * HALF, 8), HALF)
    second = pl.ds(pl.multiple_of((1 - core) * HALF, 8), HALF)
    far = lax.rem(at + 2, 4)
    slots_ref[far, first, :] = far_ref[...]
    slots_ref[far, second, :] = other_far_ref[...]
    own, got = lax.rem(at + 3 - 2 * odd, 4), lax.rem(at + 1 + 2 * odd, 4)
    slots_ref[own, first, :] = sides[0][...]
    slots_ref[own, second, :] = sides[1][...]
    slots_ref[got, first, :] = sides[2][...]
    slots_ref[got, second, :] = sides[3][...]


def fill(slots_ref, at, core, mine_ref, side_ref, other_side_ref, far_ref, other_far_ref):
    slots_ref[at] = mine_ref[...]
    slots_ref[lax.rem(at + 1 + 2 * core, 4)] = side_ref[...]
    slots_ref[lax.rem(at + 3 - 2 * core, 4)] = other_side_ref[...]
    far = lax.rem(at + 2, 4)
    slots_ref[far, pl.ds(pl.multiple_of(core * HALF, 8), HALF), :] = far_ref[...]
    slots_ref[far, pl.ds(pl.multiple_of((1 - core) * HALF, 8), HALF), :] = other_far_ref[...]


def quad_at(axis, z, x):
    return x if axis == "x" else lax.div(z, 2)


def quad_kernel(axis, *refs):
    mine_ref, parts, (t_ref, half_ref, slots_ref, tb_ref) = refs[0], refs[1:-4], refs[-4:]
    _, z, x, core = me()
    if axis == "x":
        fill(slots_ref, x, core, mine_ref, *parts)
    else:
        fill_z(slots_ref, z, core, mine_ref, *parts)
    tb = compose(load(slots_ref.at[2]), load(slots_ref.at[3]))
    ta = compose(load(slots_ref.at[0]), load(slots_ref.at[1]))
    store(tb_ref, tb)
    store(t_ref, compose(ta, tb))
    store_half(half_ref, t_ref, core)


def extend(w_ref, late_m, late_v, out_ref):
    out_ref[0 : 2 * N, :] = product(w_ref[0 : 2 * N, :], late_m)
    for state in (0, 1):
        at = 2 * N + 8 * state
        offset = times_row(w_ref[N * state : N * (state + 1), :], late_v)
        out_ref[at : at + 8, :] = w_ref[at : at + 8, :] + offset


def own_core_kernel(t_ref, a_ref, row_ref, other_ref, out_ref, w_ref):
    w_ref[0:N, :] = t_ref[0:N, :]
    w_ref[N : 2 * N, :] = a_ref[1]
    w_ref[2 * N : 2 * N + 8, :] = t_ref[V : V + 8, :]
    w_ref[2 * N + 8 :, :] = jnp.broadcast_to(row_ref[1:2, :], (8, N))
    own_pair(me()[3], w_ref, other_ref, out_ref)


def own_pair_kernel(w_ref, late_ref, out_ref):
    own_pair(lax.rem(me()[1], 2), w_ref, late_ref, out_ref)


def own_pair(bit, w_ref, late_ref, out_ref):
    @pl.when(bit == 0)
    def _():
        extend(w_ref, late_ref[0:N, :], late_ref[V : V + 1, :], out_ref)

    @pl.when(bit != 0)
    def _():
        out_ref[...] = w_ref[...]


def own_quad_kernel(axis, w_ref, slots_ref, tb_ref, out_ref):
    _, z, x, _ = me()
    at = quad_at(axis, z, x)

    @pl.when(at == 0)
    def _():
        m1, v1 = slots_ref[1, 0:N, :], slots_ref[1, V : V + 1, :]
        late_m = product(m1, tb_ref[0:N, :])
        late_v = times_row(m1, tb_ref[V : V + 1, :]) + v1
        extend(w_ref, late_m, late_v, out_ref)

    @pl.when(at == 1)
    def _():
        extend(w_ref, tb_ref[0:N, :], tb_ref[V : V + 1, :], out_ref)

    @pl.when(at == 2)
    def _():
        extend(w_ref, slots_ref[3, 0:N, :], slots_ref[3, V : V + 1, :], out_ref)

    @pl.when(at == 3)
    def _():
        out_ref[...] = w_ref[...]


def last_kernel(scale, mine_ref, a, b, c, d, w_ref, end_ref, states_ref, sens_ref, slots_ref):
    y, _, _, core = me()
    fill(slots_ref, y, core, mine_ref, a, b, c, d)
    lam = end_ref[...]
    here = lam
    total = jnp.zeros((1, G), F32)
    for q in (3, 2, 1, 0):
        here = jnp.where(y == q, lam, here)
        m, s, v, const = load(slots_ref.at[q])
        total = total + times_row(s, lam) + const
        lam = times_row(m, lam) + v
    sens_ref[...] = total * scale
    for state in (0, 1):
        at = 2 * N + 8 * state
        states_ref[state : state + 1, :] = (
            times_row(w_ref[N * state : N * (state + 1), :], here) + w_ref[at : at + 1, :]
        )


def call(kernel, outs, args, scratch=(), products=1):
    shapes = [jax.ShapeDtypeStruct(o, F32) for o in outs]
    return pl.pallas_call(
        kernel,
        out_shape=shapes,
        in_specs=[VM] * len(args),
        out_specs=[VM] * len(outs),
        scratch_shapes=list(scratch),
        compiler_params=pltpu.CompilerParams(vmem_limit_bytes=16 << 20),
        cost_estimate=pl.CostEstimate(
            flops=products * 6 * MS * N * N, bytes_accessed=1 << 20, transcendentals=0
        ),
    )(*args)


def send(value, move):
    return lax.ppermute(value, "tm", move)


def gather(whole, half, moves):
    side, far = send(whole, moves[0]), send(half, moves[1])
    return side, send(side, OTHER_CORE), far, send(far, OTHER_CORE)


def local(step_ops, sources, terminal, inertia_jac, gen_bus):
    t, h, w = (ROWS, N), (HALF, N), (W_ROWS, N)
    part = functools.partial
    wide = lambda rows: jnp.pad(rows, ((0, 0), (0, N - G)))
    rows = jnp.concatenate(
        [sources, wide(inertia_jac), wide(gen_bus.astype(F32).reshape(1, G)), jnp.zeros((3, N), F32)]
    )
    (leaf,) = call(leaf_kernel, [t], [step_ops, rows])
    total = leaf
    other = send(total, OTHER_CORE)
    total, half = call(core_kernel, [t, h], [total, other])

    parts = gather(total, half, X_FROM)
    (own,) = call(own_core_kernel, [w], [leaf, step_ops, rows, other], scratch=[pltpu.VMEM(w, F32)])
    total, half, slots, tb = call(
        part(quad_kernel, "x"), [t, h, (4,) + t, t], [total, *parts], products=3
    )

    direct = send(half, Z_ONE)
    swapped = send(direct, OTHER_CORE)
    (own,) = call(part(own_quad_kernel, "x"), [w], [own, slots, tb], products=2)
    total, half, late = call(pair_kernel, [t, h, t], [total, direct, swapped])

    side, far = send(half, Z_SIDE), send(half, Z_FAR)
    got = send(side, Z_ONE)
    parts = [far, send(far, OTHER_CORE)]
    for part_ in (side, got):
        parts += [part_, send(part_, OTHER_CORE)]
    (own,) = call(own_pair_kernel, [w], [own, late])
    total, half, slots, tb = call(
        part(quad_kernel, "z"), [t, h, (4,) + t, t], [total, *parts], products=3
    )

    parts = gather(total, half, Y_FROM)
    (own,) = call(part(own_quad_kernel, "z"), [w], [own, slots, tb], products=2)
    steps = step_ops.shape[0] * lax.axis_size("tm")
    states, sens = call(
        part(last_kernel, float(steps) ** -0.5),
        [(2, N), (1, G)],
        [total, *parts, own, terminal.reshape(1, N)],
        scratch=[pltpu.VMEM((4,) + t, F32)],
    )
    return states, sens.reshape(G)


def solution(mesh):
    in_specs = (P("tm", None, None), P("tm", None), P(), P("tm", None), P())
    out_specs = (P("tm", None), P())
    return jax.shard_map(local, mesh=mesh, in_specs=in_specs, out_specs=out_specs, check_vma=False)
```
